32 devices in a mesh: dp: 2 (over x), row: 4 (over y, core), col: 4 (over z).
Axes of the slice: x: 2, y: 2, z: 4, core: 2. Of those that a mesh axis runs over, the one named last changes fastest.
Arguments:
- tokens: bfloat16 [256, 4096], P(('dp', 'col'), 'row'), may hold values from -6 to 6
- up_weight: bfloat16 [4096, 8192], P('row', 'col'), may hold values from -0.09375 to 0.09375
- up_bias: float32 [8192], P('col'), may hold values from -3 to 3
- down_weight: bfloat16 [8192, 4096], P('col', 'row'), may hold values from -0.0625 to 0.0625
- out_grad: bfloat16 [256, 4096], P(('dp', 'col'), 'row'), may hold values from -6 to 6
- bucket_lengths: int32 [8], P(('dp', 'col')), may hold values from 1 to 32, as said below
Outputs:
- input_grad: bfloat16 [256, 4096], P(('dp', 'col'), 'row')
- up_weight_grad: float32 [4096, 4, 2048], P('row', 'col', 'dp')
- up_bias_grad: float32 [4, 2048], P('col', 'dp')
- down_weight_grad: float32 [4, 2048, 4096], P('col', 'dp', 'row')
The draws below stay inside these ranges and needn't reach their ends.
Inputs may be any that keep to these rules, and one draw needn't show every extreme that they name: `bucket_lengths`: some block is full.
All inputs are finite; a program needn't handle non-finite values.
Results may differ from the reference program's by a relative error of at most 0.0055.
Values may be sent and summed in bfloat16 or wider, within the bound.
A program may use at most 128 MiB of HBM per device.

```python
import math
import jax
import jax.numpy as jnp
from jax import lax

D = 4096
FF = 8192
CAP = 32
TOKENS = 256
FF_TILE = 2048
N_COL = 4


def draw_bucket_lengths(key, part):
    count = TOKENS // CAP
    first_key = jax.random.fold_in(key, 11)
    second_key = jax.random.fold_in(key, 23)
    lengths = jax.random.randint(first_key, (count,), 1, CAP + 1, dtype=jnp.int32)
    full_block = jax.random.randint(second_key, (), 0, count, dtype=jnp.int32)
    return jnp.where(jnp.arange(count, dtype=jnp.int32) == full_block, CAP, lengths).astype(jnp.int32)


def level_of(own_key, shape, split, low, high):
    level, own = 1.0, jax.random.fold_in(own_key, 6)
    for dim, blocks in split:
        steps = jnp.exp(jax.random.uniform(jax.random.fold_in(own, dim), (blocks,), jnp.float32, low / len(split), high / len(split)))
        level = level * jnp.repeat(steps, shape[dim] // blocks).reshape([-1 if axis == dim else 1 for axis in range(len(shape))])
    return level


def normal_values(rng, shape, width, bound, pieces=(), kind=jnp.bfloat16):
    loudness = level_of(rng, shape, pieces, -0.22, 0.18) if pieces else 1.0
    result = jax.random.normal(rng, shape, jnp.float32) * width * loudness
    return jnp.minimum(jnp.maximum(result, -bound), bound).astype(kind)


def setup_inputs(seed: int = 0) -> dict:
    seeds = jax.random.split(jax.random.key(seed), 7)
    tokens = normal_values(seeds[0], (TOKENS, D), 1.0, 6.0, ((0, 8), (1, 4)))
    up_weight = normal_values(seeds[1], (D, FF), D ** -0.5, 0.09375, ((0, 4), (1, 4)))
    up_bias = normal_values(seeds[2], (FF,), 0.5, 3.0, ((0, 4),), jnp.float32)
    down_weight = normal_values(seeds[3], (FF, D), FF ** -0.5, 0.0625, ((0, 4), (1, 4)))
    out_grad = normal_values(seeds[4], (TOKENS, D), 1.0, 6.0, ((0, 8), (1, 4)))
    bucket_lengths = draw_bucket_lengths(jax.random.fold_in(seeds[6], 71), 0)
    return dict(tokens=tokens, up_weight=up_weight, up_bias=up_bias, down_weight=down_weight, out_grad=out_grad, bucket_lengths=bucket_lengths)


coef = math.sqrt(2.0 / math.pi)

def gelu_pair(pre):
    inner = coef * (pre + 0.044715 * pre * pre * pre)
    tanh_val = jnp.tanh(inner)
    value = 0.5 * pre * (1.0 + tanh_val)
    slope = 0.5 * (1.0 + tanh_val) + 0.5 * pre * (1.0 - tanh_val * tanh_val) * coef * (1.0 + 3.0 * 0.044715 * pre * pre)
    return (value, slope)

def reference(tokens, up_weight, up_bias, down_weight, out_grad, bucket_lengths):
    position = jnp.arange(TOKENS, dtype=jnp.int32)
    limits = jnp.repeat(bucket_lengths, CAP, total_repeat_length=TOKENS)
    live = position % CAP < limits
    masked = jnp.where(live[:, None], out_grad, jnp.zeros_like(out_grad))
    pre = jnp.dot(tokens, up_weight, preferred_element_type=jnp.float32) + up_bias[None, :]
    value, slope = gelu_pair(pre)
    act = value.astype(jnp.bfloat16)
    act_grad = jnp.dot(masked, down_weight.T, preferred_element_type=jnp.float32)
    pre_grad = (act_grad * slope).astype(jnp.bfloat16)
    down_grad = jnp.dot(act.T, masked, preferred_element_type=jnp.float32)
    up_grad = jnp.dot(tokens.T, pre_grad, preferred_element_type=jnp.float32)
    bias_grad = lax.optimization_barrier(jnp.sum(pre_grad.astype(jnp.float32), axis=0))
    input_grad = jnp.dot(pre_grad, up_weight.T, preferred_element_type=jnp.float32).astype(jnp.bfloat16)
    return (input_grad, up_grad.reshape(D, N_COL, FF_TILE), bias_grad.reshape(N_COL, FF_TILE), down_grad.reshape(N_COL, FF_TILE, D))
```

```python
import functools
import math

import jax
import jax.numpy as jnp
from jax import lax
from jax.experimental import pallas as pl
from jax.experimental.pallas import tpu as pltpu
from jax.sharding import PartitionSpec as P

coef = math.sqrt(2.0 / math.pi)
MESH = pl.DeviceIdType.MESH
BLOCKS = 2


def gelu_pair(pre):
    inner = coef * (pre + 0.044715 * pre * pre * pre)
    tanh_val = jnp.tanh(inner)
    value = 0.5 * pre * (1.0 + tanh_val)
    slope = 0.5 * (1.0 + tanh_val) + 0.5 * pre * (1.0 - tanh_val * tanh_val) * coef * (
        1.0 + 3.0 * 0.044715 * pre * pre
    )
    return (value, slope)


def contract_rows(left, right):
    return lax.dot_general(
        left, right, (((0,), (0,)), ((), ())), preferred_element_type=jnp.float32
    )


def contract_cols(left, right):
    return lax.dot_general(
        left, right, (((1,), (1,)), ((), ())), preferred_element_type=jnp.float32
    )


def flip(index, bits):
    bit = 1
    out = index
    while bit <= bits:
        if bits & bit:
            out = out + bit - 2 * bit * ((index // bit) % 2)
        bit *= 2
    return out


def exchange(
    n_dp, n_row, n_col,
    tok_ref, og_ref, len_ref, bias_ref, wup_hbm, wdn_hbm,
    ig_ref, feats_out, grads_out, act_out, pg_out,
    xg, wup, wdn, part, sent, core_in, mid, row_in, ap, igs, igf, x_in, zs, zr,
    w_sem, own_sem, out_sem, act_sem, ag_send_r, ag_send_l, ag_send_x, ag_recv,
    core_sem, row_sem, pair_sem, igx_send, igx_recv, z_send, z_recv,
):
    dp, row, col = lax.axis_index("dp"), lax.axis_index("row"), lax.axis_index("col")
    bl, width = tok_ref.shape
    blocks = len_ref.shape[0]
    hs = wup.shape[1]
    S = BLOCKS
    nch = n_col // S
    slab = n_dp * bl
    rows = S * slab
    half = rows // 2
    tile = min(256, hs)
    first = pl.multiple_of(dp * hs, hs)
    mate = flip(row, 1)
    mine = row % 2
    far_bits = [1 << b for b in range(1, n_row.bit_length() - 1)]
    pending = []

    w_copies = [
        pltpu.make_async_copy(wup_hbm.at[:, pl.ds(first, hs)], wup, w_sem.at[0]),
        pltpu.make_async_copy(wdn_hbm.at[pl.ds(first, hs), :], wdn, w_sem.at[1]),
    ]
    for copy in w_copies:
        copy.start()

    def group(g):
        return pl.ds(pl.multiple_of(g * bl, bl), bl)

    def block(c, g):
        return xg.at[:, c, group(g), :]

    barrier = pltpu.get_barrier_semaphore()
    peers = [{"dp": (dp + p) % n_dp} for p in range(1, n_dp)]
    peers += [{"col": (col + p) % n_col} for p in range(1, n_col)]
    peers += [{"row": mate}] + [{"row": flip(row, bits)} for bits in far_bits]
    for peer in peers:
        pl.semaphore_signal(barrier, inc=1, device_id=peer, device_id_type=MESH)
    xg[0, col, group(dp), :] = tok_ref[...]
    spot = lax.broadcasted_iota(jnp.int32, (bl, width), 0)
    live = spot < len_ref[0]
    for k in range(1, blocks):
        start = k * (bl // blocks)
        live = jnp.where(spot < start, live, spot - start < len_ref[k])
    out_grad = og_ref[...].astype(jnp.float32)
    xg[1, col, group(dp), :] = jnp.where(live, out_grad, jnp.zeros_like(out_grad)).astype(jnp.bfloat16)
    pl.semaphore_wait(barrier, len(peers))

    def remote(src, dst, send, recv, dev):
        return pltpu.make_async_remote_copy(
            src_ref=src, dst_ref=dst, send_sem=send, recv_sem=recv,
            device_id=dev, device_id_type=MESH,
        )

    def go(copy, cond=None):
        if cond is None:
            copy.start()
        else:
            pl.when(cond)(copy.start)
        pending.append((copy, cond))

    def give(src, c, p):
        return remote(
            src, block(c, dp), ag_send_x.at[p, c], ag_recv.at[dp, c],
            {"dp": (dp + p) % n_dp},
        )

    def send_line(s, src_of):
        low = jnp.maximum(col - s, 0)
        high = jnp.minimum(col + s, n_col - 1)
        if s < n_col - 1:
            right = jnp.minimum(col + 1, n_col - 1)
            left = jnp.maximum(col - 1, 0)
            ok_r = jnp.logical_and(col - s >= 0, col + 1 < n_col)
            ok_l = jnp.logical_and(col + s < n_col, col >= 1)
            go(remote(src_of(low), block(low, dp), ag_send_r.at[s], ag_recv.at[dp, low],
                      {"col": right}), ok_r)
            go(remote(src_of(high), block(high, dp), ag_send_l.at[s], ag_recv.at[dp, high],
                      {"col": left}), ok_l)

    def forward(s):
        low = jnp.maximum(col - s, 0)
        high = jnp.minimum(col + s, n_col - 1)
        for c, cond in ((low, col - s >= 0), (high, col + s < n_col)):
            wait = remote(block(c, dp), block(c, dp), own_sem, ag_recv.at[dp, c], {"col": col})
            pl.when(cond)(wait.wait_recv)
        send_line(s, lambda c: block(c, dp))
        for c, cond in ((low, col - s >= 0), (high, col + s < n_col)):
            for p in range(1, n_dp):
                go(give(block(c, dp), c, p), cond)

    send_line(0, lambda c: block(c, dp))
    for p in range(1, n_dp):
        go(give(block(col, dp), col, p))

    def base(j):
        return S * flip(col // S, j)

    def lanes(n):
        return pl.ds(pl.multiple_of(n * tile, tile), tile)

    def my_half(which):
        return pl.ds(pl.multiple_of(which * half, half), half)

    def stage_a(j):
        for i in range(S):
            c = base(j) + i
            for p in range(1, n_dp):
                g = (dp + p) % n_dp
                remote(block(c, g), block(c, g), own_sem, ag_recv.at[g, c], {"dp": g}).wait_recv()
        if j == 0:
            for copy in w_copies:
                copy.wait()
        b = base(j)

        @pl.loop(0, hs // tile)
        def _(n):
            feats = xg[0, pl.ds(b, S)].reshape(rows, width)
            grads = xg[1, pl.ds(b, S)].reshape(rows, width)
            up = jnp.dot(feats, wup[:, lanes(n)], preferred_element_type=jnp.float32)
            part[j, 0, :, lanes(n)] = up
            sent[j, 0, :, lanes(n)] = up.astype(jnp.bfloat16)
            down = contract_cols(grads, wdn[lanes(n), :])
            part[j, 1, :, lanes(n)] = down
            sent[j, 1, :, lanes(n)] = down.astype(jnp.bfloat16)

        go(remote(sent.at[j, :, my_half(1 - mine), :], core_in.at[j],
                  core_sem.at[0, j], core_sem.at[1, j], {"row": mate}))

    def stage_b(j):
        remote(core_in.at[j], core_in.at[j], own_sem, core_sem.at[1, j], {"row": mate}).wait_recv()

        @pl.loop(0, hs // tile)
        def _(n):
            for k in range(2):
                total = part[j, k, my_half(mine), lanes(n)] + core_in[j, k, :, lanes(n)].astype(jnp.float32)
                mid[j, 0, k, :, lanes(n)] = total.astype(jnp.bfloat16)

        go(remote(mid.at[j, 0], row_in.at[j, 0], row_sem.at[0, j, 0], row_sem.at[1, j, 0],
                  {"row": flip(row, far_bits[0])}))

    def stage_c(j):
        for i, bits in enumerate(far_bits):
            remote(row_in.at[j, i], row_in.at[j, i], own_sem, row_sem.at[1, j, i],
                   {"row": mate}).wait_recv()
            if i + 1 < len(far_bits):
                mid[j, i + 1] = (mid[j, i].astype(jnp.float32) + row_in[j, i].astype(jnp.float32)).astype(jnp.bfloat16)
                go(remote(mid.at[j, i + 1], row_in.at[j, i + 1], row_sem.at[0, j, i + 1],
                          row_sem.at[1, j, i + 1], {"row": flip(row, far_bits[i + 1])}))
        last = len(far_bits) - 1

        @pl.loop(0, hs // tile)
        def _(n):
            pre = mid[j, last, 0, :, lanes(n)].astype(jnp.float32) + row_in[j, last, 0, :, lanes(n)].astype(jnp.float32)
            grad = mid[j, last, 1, :, lanes(n)].astype(jnp.float32) + row_in[j, last, 1, :, lanes(n)].astype(jnp.float32)
            bias = bias_ref[:, pl.ds(pl.multiple_of(dp * hs + n * tile, tile), tile)]
            value, slope = gelu_pair(pre + bias)
            ap[0, j, my_half(mine), lanes(n)] = value.astype(jnp.bfloat16)
            ap[1, j, my_half(mine), lanes(n)] = (grad * slope).astype(jnp.bfloat16)

        here = ap.at[:, j, my_half(mine), :]
        go(remote(here, here, pair_sem.at[0, j], pair_sem.at[1, j], {"row": mate}))

    def stage_d(j):
        there = ap.at[:, j, my_half(1 - mine), :]
        remote(there, there, own_sem, pair_sem.at[1, j], {"row": mate}).wait_recv()

        @pl.loop(0, width // 256)
        def _(n):
            cols = pl.ds(pl.multiple_of(n * 256, 256), 256)
            res = contract_cols(ap[1, j], wup[cols, :])
            igf[j, :, :, cols] = res.reshape(S, slab, 256)
            igs[j, :, :, cols] = res.astype(jnp.bfloat16).reshape(S, slab, 256)

        for p in range(1, n_dp):
            g = (dp + p) % n_dp
            go(remote(igs.at[j, :, group(g), :], x_in.at[j, p], igx_send.at[j, p], igx_recv.at[j, p],
                      {"dp": g}))

    def stage_e(j):
        for p in range(1, n_dp):
            remote(x_in.at[j, p], x_in.at[j, p], own_sem, igx_recv.at[j, p], {"dp": dp}).wait_recv()
        total = igf[j, :, group(dp), :]
        for p in range(1, n_dp):
            total = total + x_in[j, p].astype(jnp.float32)
        zs[j] = total.astype(jnp.bfloat16)
        if j == 0:
            igf[j, :, group(dp), :] = total
        offs = range(1, S) if j == 0 else range(S)
        for i in offs:
            at = (col + i) % S
            c = base(j) + at
            go(remote(zs.at[j, at], zr.at[col], z_send.at[j, i], z_recv.at[col], {"col": c}))

    out_copies = [
        pltpu.make_async_copy(xg.at[0], feats_out, out_sem.at[0]),
        pltpu.make_async_copy(xg.at[1], grads_out, out_sem.at[1]),
    ]
    act_copies = []
    for j in range(nch):
        at = base(j) // S
        act_copies.append(pltpu.make_async_copy(ap.at[0, j], act_out.at[at], act_sem.at[0, j]))
        act_copies.append(pltpu.make_async_copy(ap.at[1, j], pg_out.at[at], act_sem.at[1, j]))

    forward(1)
    if n_col > 2:
        forward(2)
    for t in range(nch + 2):
        if t < nch:
            if t == 1:
                for s in range(3, n_col):
                    forward(s)
            stage_a(t)
            if t == nch - 1:
                for copy in out_copies:
                    copy.start()
        if 0 <= t - 1 < nch:
            if t < nch:
                stage_b(t)
            stage_c(t - 1)
            stage_d(t - 1)
            for copy in act_copies[2 * t - 2 : 2 * t]:
                copy.start()
        elif t < nch:
            stage_b(t)
        if 0 <= t - 2 < nch:
            stage_e(t - 2)
    total = igf[0, col % S, group(dp), :]
    for p in range(1, n_col):
        c = (col + p) % n_col
        remote(zr.at[c], zr.at[c], own_sem, z_recv.at[c], {"col": c}).wait_recv()
        total = total + zr[c].astype(jnp.float32)
    ig_ref[...] = total.astype(jnp.bfloat16)
    for copy, cond in pending:
        if cond is None:
            copy.wait_send()
        else:
            pl.when(cond)(copy.wait_send)
    for copy in out_copies + act_copies:
        copy.wait()


def grads_kernel(feats_ref, pg_ref, act_ref, grads_ref, up_ref, bias_ref, down_ref):
    @pl.when(pl.program_id(0) == 0)
    def _():
        bias_ref[...] = jnp.sum(pg_ref[...].astype(jnp.float32), axis=0, keepdims=True)

    hs = pg_ref.shape[1]
    up = contract_rows(feats_ref[...], pg_ref[...])
    for k in range(hs // 128):
        up_ref[:, k, :] = up[:, k * 128 : (k + 1) * 128]
    down_ref[0] = contract_rows(act_ref[...], grads_ref[...])


def weight_grads(feats, grads, act, pg):
    rows, width = feats.shape
    hs = pg.shape[1]
    steps = max(1, hs // 256)
    f32 = jnp.float32
    return pl.pallas_call(
        grads_kernel,
        grid=(steps,),
        out_shape=(
            jax.ShapeDtypeStruct((width, hs // 128, 128), f32),
            jax.ShapeDtypeStruct((1, hs), f32),
            jax.ShapeDtypeStruct((1, hs, width), f32),
        ),
        in_specs=[
            pl.BlockSpec((rows, width // steps), lambda i: (0, i)),
            pl.BlockSpec((rows, hs), lambda i: (0, 0)),
            pl.BlockSpec((rows, hs // steps), lambda i: (0, i)),
            pl.BlockSpec((rows, width), lambda i: (0, 0)),
        ],
        out_specs=(
            pl.BlockSpec((width // steps, hs // 128, 128), lambda i: (i, 0, 0)),
            pl.BlockSpec((1, hs), lambda i: (0, 0)),
            pl.BlockSpec((1, hs // steps, width), lambda i: (0, i, 0)),
        ),
        compiler_params=pltpu.CompilerParams(vmem_limit_bytes=48 * 1024 * 1024),
    )(feats, pg, act, grads)


def local(n_dp, n_row, n_col, tokens, up_weight, up_bias, down_weight, out_grad, bucket_lengths):
    bl, width = out_grad.shape
    hidden = up_weight.shape[1]
    hs = hidden // n_dp
    S = BLOCKS
    nch = n_col // S
    slab = n_dp * bl
    rows = S * slab
    far = n_row.bit_length() - 2
    bf, f32 = jnp.bfloat16, jnp.float32
    VM, DMA = pltpu.VMEM, pltpu.SemaphoreType.DMA
    vmem = pl.BlockSpec(memory_space=pltpu.VMEM)
    smem = pl.BlockSpec(memory_space=pltpu.SMEM)
    hbm = pl.BlockSpec(memory_space=pl.ANY)
    input_grad, feats, grads, act, pg = pl.pallas_call(
        functools.partial(exchange, n_dp, n_row, n_col),
        out_shape=(
            jax.ShapeDtypeStruct((bl, width), bf),
            jax.ShapeDtypeStruct((n_col, slab, width), bf),
            jax.ShapeDtypeStruct((n_col, slab, width), bf),
            jax.ShapeDtypeStruct((nch, rows, hs), bf),
            jax.ShapeDtypeStruct((nch, rows, hs), bf),
        ),
        in_specs=[vmem, vmem, smem, vmem, hbm, hbm],
        out_specs=(vmem, hbm, hbm, hbm, hbm),
        scratch_shapes=[
            VM((2, n_col, slab, width), bf),
            VM((width, hs), bf),
            VM((hs, width), bf),
            VM((nch, 2, rows, hs), f32),
            VM((nch, 2, rows, hs), bf),
            VM((nch, 2, rows // 2, hs), bf),
            VM((nch, far, 2, rows // 2, hs), bf),
            VM((nch, far, 2, rows // 2, hs), bf),
            VM((2, nch, rows, hs), bf),
            VM((nch, S, slab, width), bf),
            VM((nch, S, slab, width), f32),
            VM((nch, n_dp, S, bl, width), bf),
            VM((nch, S, bl, width), bf),
            VM((n_col, bl, width), bf),
            DMA((2,)), DMA(()), DMA((2,)), DMA((2, nch)),
            DMA((n_col,)), DMA((n_col,)), DMA((n_dp, n_col)), DMA((n_dp, n_col)),
            DMA((2, nch)), DMA((2, nch, far)), DMA((2, nch)),
            DMA((nch, n_dp)), DMA((nch, n_dp)), DMA((nch, S)), DMA((n_col,)),
        ],
        compiler_params=pltpu.CompilerParams(
            collective_id=0, has_side_effects=True, vmem_limit_bytes=60 * 1024 * 1024
        ),
    )(tokens, out_grad, bucket_lengths, up_bias.reshape(1, hidden), up_weight, down_weight)
    feats = feats.reshape(n_col * slab, width)
    grads = grads.reshape(n_col * slab, width)
    act = act.reshape(n_col * slab, hs)
    pg = pg.reshape(n_col * slab, hs)
    up_grad, bias_grad, down_grad = weight_grads(feats, grads, act, pg)
    return (
        input_grad,
        up_grad.reshape(width, 1, hs),
        bias_grad.reshape(1, hs),
        down_grad.reshape(1, hs, width),
    )


def solution(mesh):
    sizes = (mesh.shape["dp"], mesh.shape["row"], mesh.shape["col"])
    return jax.shard_map(
        functools.partial(local, *sizes),
        mesh=mesh,
        in_specs=(
            P(("dp", "col"), "row"),
            P("row", "col"),
            P("col"),
            P("col", "row"),
            P(("dp", "col"), "row"),
            P(("dp", "col")),
        ),
        out_specs=(
            P(("dp", "col"), "row"),
            P("row", "col", "dp"),
            P("col", "dp"),
            P("col", "dp", "row"),
        ),
        check_vma=False,
    )
```

```python
import functools
import math

import jax
import jax.numpy as jnp
from jax import lax
from jax.experimental import pallas as pl
from jax.experimental.pallas import tpu as pltpu
from jax.sharding import PartitionSpec as P

coef = math.sqrt(2.0 / math.pi)
MESH = pl.DeviceIdType.MESH
BLOCKS = 2


def gelu_pair(pre):
    inner = coef * (pre + 0.044715 * pre * pre * pre)
    tanh_val = jnp.tanh(inner)
    value = 0.5 * pre * (1.0 + tanh_val)
    slope = 0.5 * (1.0 + tanh_val) + 0.5 * pre * (1.0 - tanh_val * tanh_val) * coef * (
        1.0 + 3.0 * 0.044715 * pre * pre
    )
    return (value, slope)


def contract_rows(left, right):
    return lax.dot_general(
        left, right, (((0,), (0,)), ((), ())), preferred_element_type=jnp.float32
    )


def contract_cols(left, right):
    return lax.dot_general(
        left, right, (((1,), (1,)), ((), ())), preferred_element_type=jnp.float32
    )


def flip(index, bits):
    bit = 1
    out = index
    while bit <= bits:
        if bits & bit:
            out = out + bit - 2 * bit * ((index // bit) % 2)
        bit *= 2
    return out


def exchange(
    n_dp, n_row, n_col,
    tok_ref, og_ref, len_ref, bias_ref, wup_hbm, wdn_hbm,
    ig_ref, feats_out, grads_out, act_out, pg_out,
    xg, wup, wdn, part, sent, core_in, mid, row_in, ap, igs, igf, x_in, zs, zr,
    w_sem, own_sem, out_sem, act_sem, ag_send_r, ag_send_l, ag_send_x, ag_recv,
    core_sem, row_sem, pair_sem, igx_send, igx_recv, z_send, z_recv,
):
    dp, row, col = lax.axis_index("dp"), lax.axis_index("row"), lax.axis_index("col")
    bl, width = tok_ref.shape
    blocks = len_ref.shape[0]
    hs = wup.shape[1]
    S = BLOCKS
    nch = n_col // S
    slab = n_dp * bl
    rows = S * slab
    half = rows // 2
    tile = min(256, hs)
    first = pl.multiple_of(dp * hs, hs)
    mate = flip(row, 1)
    mine = row % 2
    far_bits = [1 << b for b in range(1, n_row.bit_length() - 1)]
    pending = []

    w_copies = [
        pltpu.make_async_copy(wup_hbm.at[:, pl.ds(first, hs)], wup, w_sem.at[0]),
        pltpu.make_async_copy(wdn_hbm.at[pl.ds(first, hs), :], wdn, w_sem.at[1]),
    ]
    for copy in w_copies:
        copy.start()

    def group(g):
        return pl.ds(pl.multiple_of(g * bl, bl), bl)

    def block(k, c, g):
        return xg.at[k, c, group(g), :]

    barrier = pltpu.get_barrier_semaphore()
    peers = [{"dp": (dp + p) % n_dp} for p in range(1, n_dp)]
    peers += [{"row": mate}] + [{"row": flip(row, bits)} for bits in far_bits]
    for peer in peers:
        pl.semaphore_signal(barrier, inc=1, device_id=peer, device_id_type=MESH)
    has_r, has_l = col + 1 < n_col, col >= 1
    step_r, step_l = jnp.minimum(col + 1, n_col - 1), jnp.maximum(col - 1, 0)
    for cond, c in ((has_r, step_r), (has_l, step_l)):
        @pl.when(cond)
        def _():
            pl.semaphore_signal(barrier, inc=1, device_id={"col": c}, device_id_type=MESH)
    xg[0, col, group(dp), :] = tok_ref[...]
    spot = lax.broadcasted_iota(jnp.int32, (bl, width), 0)
    live = spot < len_ref[0]
    for k in range(1, blocks):
        start = k * (bl // blocks)
        live = jnp.where(spot < start, live, spot - start < len_ref[k])
    out_grad = og_ref[...].astype(jnp.float32)
    xg[1, col, group(dp), :] = jnp.where(live, out_grad, jnp.zeros_like(out_grad)).astype(jnp.bfloat16)
    beside = jnp.minimum(n_col - 1 - col, 1) + jnp.minimum(col, 1)
    pl.semaphore_wait(barrier, len(peers) + beside)

    def remote(src, dst, send, recv, dev):
        return pltpu.make_async_remote_copy(
            src_ref=src, dst_ref=dst, send_sem=send, recv_sem=recv,
            device_id=dev, device_id_type=MESH,
        )

    def go(copy, cond=None):
        if cond is None:
            copy.start()
        else:
            pl.when(cond)(copy.start)
        pending.append((copy, cond))

    def give(k, c, p):
        return remote(
            block(k, c, dp), block(k, c, dp), ag_send_x.at[k, p, c], ag_recv.at[k, dp, c],
            {"dp": (dp + p) % n_dp},
        )

    def arrived(k, c, g):
        return remote(block(k, c, g), block(k, c, g), own_sem, ag_recv.at[k, g, c], {"col": col})

    def forward(s):
        low = jnp.maximum(col - s, 0)
        high = jnp.minimum(col + s, n_col - 1)
        has_low, has_high = col - s >= 0, col + s < n_col
        for k in range(2):
            for c, cond, edge, to, sems in (
                (low, has_low, has_r, step_r, ag_send_r),
                (high, has_high, has_l, step_l, ag_send_l),
            ):
                if s > 0:
                    pl.when(cond)(arrived(k, c, dp).wait_recv)
                if s < n_col - 1:
                    go(remote(block(k, c, dp), block(k, c, dp), sems.at[k, s],
                              ag_recv.at[k, dp, c], {"col": to}), jnp.logical_and(cond, edge))
            if s == 0:
                for p in range(1, n_dp):
                    go(give(k, col, p))
            else:
                for c, cond in ((low, has_low), (high, has_high)):
                    for p in range(1, n_dp):
                        go(give(k, c, p), cond)

    forward(0)

    def base(j):
        return S * flip(col // S, j)

    def lanes(n):
        return pl.ds(pl.multiple_of(n * tile, tile), tile)

    def my_half(which):
        return pl.ds(pl.multiple_of(which * half, half), half)

    def stage_a(j):
        for i in range(S):
            c = base(j) + i
            for p in range(1, n_dp):
                g = (dp + p) % n_dp
                for k in range(2):
                    arrived(k, c, g).wait_recv()
        if j == 0:
            for copy in w_copies:
                copy.wait()
        b = base(j)

        @pl.loop(0, hs // tile)
        def _(n):
            feats = xg[0, pl.ds(b, S)].reshape(rows, width)
            grads = xg[1, pl.ds(b, S)].reshape(rows, width)
            up = jnp.dot(feats, wup[:, lanes(n)], preferred_element_type=jnp.float32)
            part[j, 0, :, lanes(n)] = up
            sent[j, 0, :, lanes(n)] = up.astype(jnp.bfloat16)
            down = contract_cols(grads, wdn[lanes(n), :])
            part[j, 1, :, lanes(n)] = down
            sent[j, 1, :, lanes(n)] = down.astype(jnp.bfloat16)

        go(remote(sent.at[j, :, my_half(1 - mine), :], core_in.at[j],
                  core_sem.at[0, j], core_sem.at[1, j], {"row": mate}))

    def stage_b(j):
        remote(core_in.at[j], core_in.at[j], own_sem, core_sem.at[1, j], {"row": mate}).wait_recv()

        @pl.loop(0, hs // tile)
        def _(n):
            for k in range(2):
                total = part[j, k, my_half(mine), lanes(n)] + core_in[j, k, :, lanes(n)].astype(jnp.float32)
                mid[j, 0, k, :, lanes(n)] = total.astype(jnp.bfloat16)

        go(remote(mid.at[j, 0], row_in.at[j, 0], row_sem.at[0, j, 0], row_sem.at[1, j, 0],
                  {"row": flip(row, far_bits[0])}))

    def stage_c(j):
        for i, bits in enumerate(far_bits):
            remote(row_in.at[j, i], row_in.at[j, i], own_sem, row_sem.at[1, j, i],
                   {"row": mate}).wait_recv()
            if i + 1 < len(far_bits):
                mid[j, i + 1] = (mid[j, i].astype(jnp.float32) + row_in[j, i].astype(jnp.float32)).astype(jnp.bfloat16)
                go(remote(mid.at[j, i + 1], row_in.at[j, i + 1], row_sem.at[0, j, i + 1],
                          row_sem.at[1, j, i + 1], {"row": flip(row, far_bits[i + 1])}))
        last = len(far_bits) - 1

        @pl.loop(0, hs // tile)
        def _(n):
            pre = mid[j, last, 0, :, lanes(n)].astype(jnp.float32) + row_in[j, last, 0, :, lanes(n)].astype(jnp.float32)
            grad = mid[j, last, 1, :, lanes(n)].astype(jnp.float32) + row_in[j, last, 1, :, lanes(n)].astype(jnp.float32)
            bias = bias_ref[:, pl.ds(pl.multiple_of(dp * hs + n * tile, tile), tile)]
            value, slope = gelu_pair(pre + bias)
            ap[0, j, my_half(mine), lanes(n)] = value.astype(jnp.bfloat16)
            ap[1, j, my_half(mine), lanes(n)] = (grad * slope).astype(jnp.bfloat16)

        here = ap.at[:, j, my_half(mine), :]
        go(remote(here, here, pair_sem.at[0, j], pair_sem.at[1, j], {"row": mate}))

    def stage_d(j, other):
        i = 1 - mine if other else mine
        if other:
            there = ap.at[:, j, my_half(i), :]
            remote(there, there, own_sem, pair_sem.at[1, j], {"row": mate}).wait_recv()
        wide = min(512, width)

        @pl.loop(0, width // wide)
        def _(n):
            cols = pl.ds(pl.multiple_of(n * wide, wide), wide)
            res = contract_cols(ap[1, j, my_half(i), :], wup[cols, :])
            igf[j, i, :, cols] = res
            igs[j, i, :, cols] = res.astype(jnp.bfloat16)

        for p in range(1, n_dp):
            g = (dp + p) % n_dp
            go(remote(igs.at[j, i, group(g), :], x_in.at[j, p, i], igx_send.at[j, p, i],
                      igx_recv.at[j, p, i], {"dp": g}))

    def stage_e(j, other):
        i = 1 - mine if other else mine
        for p in range(1, n_dp):
            remote(x_in.at[j, p, i], x_in.at[j, p, i], own_sem, igx_recv.at[j, p, i], {"dp": dp}).wait_recv()
        total = igf[j, i, group(dp), :]
        for p in range(1, n_dp):
            total = total + x_in[j, p, i].astype(jnp.float32)
        zs[j, i] = total.astype(jnp.bfloat16)
        if j == 0:
            igf[j, i, group(dp), :] = total
        cond = i != col % S if j == 0 else None
        go(remote(zs.at[j, i], zr.at[col], z_send.at[j, i], z_recv.at[col], {"col": base(j) + i}), cond)

    out_copies = [
        pltpu.make_async_copy(xg.at[0], feats_out, out_sem.at[0]),
        pltpu.make_async_copy(xg.at[1], grads_out, out_sem.at[1]),
    ]
    act_copies = []
    for j in range(nch):
        at = base(j) // S
        act_copies.append(pltpu.make_async_copy(ap.at[0, j], act_out.at[at], act_sem.at[0, j]))
        act_copies.append(pltpu.make_async_copy(ap.at[1, j], pg_out.at[at], act_sem.at[1, j]))

    def finish(copies):
        for copy in copies:
            copy.start()

    steps = [(forward, s) for s in range(1, min(S + 1, n_col))]
    steps += [(stage_a, 0), (stage_b, 0)]
    for t in range(1, nch):
        if t == 1:
            steps += [(forward, s) for s in range(S + 1, n_col)]
        steps += [(stage_a, t)]
        if t == nch - 1:
            steps += [(finish, out_copies)]
        steps += [(stage_c, t - 1), (stage_b, t), (stage_d, t - 1, 0), (stage_d, t - 1, 1)]
        steps += [(finish, act_copies[2 * t - 2 : 2 * t])]
        steps += [(stage_e, t - 1, 0), (stage_e, t - 1, 1)]
    if nch == 1:
        steps += [(finish, out_copies)]
    t = nch - 1
    steps += [(stage_c, t), (stage_d, t, 0), (stage_d, t, 1), (finish, act_copies[2 * t :])]
    steps += [(stage_e, t, 0), (stage_e, t, 1)]
    for step, *args in steps:
        step(*args)
    total = igf[0, col % S, group(dp), :]
    for p in range(1, n_col):
        c = (col + p) % n_col
        remote(zr.at[c], zr.at[c], own_sem, z_recv.at[c], {"col": c}).wait_recv()
        total = total + zr[c].astype(jnp.float32)
    ig_ref[...] = total.astype(jnp.bfloat16)
    for copy, cond in pending:
        if cond is None:
            copy.wait_send()
        else:
            pl.when(cond)(copy.wait_send)
    for copy in out_copies + act_copies:
        copy.wait()


def grads_kernel(feats_ref, pg_ref, act_ref, grads_ref, ig_ref, up_ref, bias_ref, down_ref, out_ref):
    @pl.when(pl.program_id(0) == 0)
    def _():
        bias_ref[...] = jnp.sum(pg_ref[...].astype(jnp.float32), axis=0, keepdims=True)
        out_ref[...] = ig_ref[...]

    hs = pg_ref.shape[1]
    up = contract_rows(feats_ref[...], pg_ref[...])
    for k in range(hs // 128):
        up_ref[:, k, :] = up[:, k * 128 : (k + 1) * 128]
    down_ref[0] = contract_rows(act_ref[...], grads_ref[...])


def weight_grads(feats, grads, act, pg, input_grad):
    rows, width = feats.shape
    hs = pg.shape[1]
    steps = max(1, hs // 256)
    f32 = jnp.float32
    return pl.pallas_call(
        grads_kernel,
        grid=(steps,),
        out_shape=(
            jax.ShapeDtypeStruct((width, hs // 128, 128), f32),
            jax.ShapeDtypeStruct((1, hs), f32),
            jax.ShapeDtypeStruct((1, hs, width), f32),
            jax.ShapeDtypeStruct(input_grad.shape, input_grad.dtype),
        ),
        in_specs=[
            pl.BlockSpec((rows, width // steps), lambda i: (0, i)),
            pl.BlockSpec((rows, hs), lambda i: (0, 0), pipeline_mode=pl.Buffered(1)),
            pl.BlockSpec((rows, hs // steps), lambda i: (0, i)),
            pl.BlockSpec((rows, width), lambda i: (0, 0), pipeline_mode=pl.Buffered(1)),
            pl.BlockSpec(input_grad.shape, lambda i: (0, 0), pipeline_mode=pl.Buffered(1)),
        ],
        out_specs=(
            pl.BlockSpec((width // steps, hs // 128, 128), lambda i: (i, 0, 0)),
            pl.BlockSpec((1, hs), lambda i: (0, 0)),
            pl.BlockSpec((1, hs // steps, width), lambda i: (0, i, 0)),
            pl.BlockSpec(input_grad.shape, lambda i: (0, 0)),
        ),
        compiler_params=pltpu.CompilerParams(vmem_limit_bytes=63 * 1024 * 1024),
    )(feats, pg, act, grads, input_grad)


def local(n_dp, n_row, n_col, tokens, up_weight, up_bias, down_weight, out_grad, bucket_lengths):
    bl, width = out_grad.shape
    hidden = up_weight.shape[1]
    hs = hidden // n_dp
    S = BLOCKS
    nch = n_col // S
    slab = n_dp * bl
    rows = S * slab
    far = n_row.bit_length() - 2
    bf, f32 = jnp.bfloat16, jnp.float32
    VM, DMA = pltpu.VMEM, pltpu.SemaphoreType.DMA
    vmem = pl.BlockSpec(memory_space=pltpu.VMEM)
    smem = pl.BlockSpec(memory_space=pltpu.SMEM)
    hbm = pl.BlockSpec(memory_space=pl.ANY)
    input_grad, feats, grads, act, pg = pl.pallas_call(
        functools.partial(exchange, n_dp, n_row, n_col),
        out_shape=(
            jax.ShapeDtypeStruct((bl, width), bf),
            jax.ShapeDtypeStruct((n_col, slab, width), bf),
            jax.ShapeDtypeStruct((n_col, slab, width), bf),
            jax.ShapeDtypeStruct((nch, rows, hs), bf),
            jax.ShapeDtypeStruct((nch, rows, hs), bf),
        ),
        in_specs=[vmem, vmem, smem, vmem, hbm, hbm],
        out_specs=(vmem, hbm, hbm, hbm, hbm),
        scratch_shapes=[
            VM((2, n_col, slab, width), bf),
            VM((width, hs), bf),
            VM((hs, width), bf),
            VM((nch, 2, rows, hs), f32),
            VM((nch, 2, rows, hs), bf),
            VM((nch, 2, rows // 2, hs), bf),
            VM((nch, far, 2, rows // 2, hs), bf),
            VM((nch, far, 2, rows // 2, hs), bf),
            VM((2, nch, rows, hs), bf),
            VM((nch, S, slab, width), bf),
            VM((nch, S, slab, width), f32),
            VM((nch, n_dp, S, bl, width), bf),
            VM((nch, S, bl, width), bf),
            VM((n_col, bl, width), bf),
            DMA((2,)), DMA(()), DMA((2,)), DMA((2, nch)),
            DMA((2, n_col)), DMA((2, n_col)), DMA((2, n_dp, n_col)), DMA((2, n_dp, n_col)),
            DMA((2, nch)), DMA((2, nch, far)), DMA((2, nch)),
            DMA((nch, n_dp, S)), DMA((nch, n_dp, S)), DMA((nch, S)), DMA((n_col,)),
        ],
        compiler_params=pltpu.CompilerParams(
            collective_id=0, has_side_effects=True, vmem_limit_bytes=60 * 1024 * 1024
        ),
    )(tokens, out_grad, bucket_lengths, up_bias.reshape(1, hidden), up_weight, down_weight)
    feats = feats.reshape(n_col * slab, width)
    grads = grads.reshape(n_col * slab, width)
    act = act.reshape(n_col * slab, hs)
    pg = pg.reshape(n_col * slab, hs)
    up_grad, bias_grad, down_grad, input_grad = weight_grads(feats, grads, act, pg, input_grad)
    return (
        input_grad,
        up_grad.reshape(width, 1, hs),
        bias_grad.reshape(1, hs),
        down_grad.reshape(1, hs, width),
    )


def solution(mesh):
    sizes = (mesh.shape["dp"], mesh.shape["row"], mesh.shape["col"])
    return jax.shard_map(
        functools.partial(local, *sizes),
        mesh=mesh,
        in_specs=(
            P(("dp", "col"), "row"),
            P("row", "col"),
            P("col"),
            P("col", "row"),
            P(("dp", "col"), "row"),
            P(("dp", "col")),
        ),
        out_specs=(
            P(("dp", "col"), "row"),
            P("row", "col", "dp"),
            P("col", "dp"),
            P("col", "dp", "row"),
        ),
        check_vma=False,
    )
```

```python
import functools
import math

import jax
import jax.numpy as jnp
from jax import lax
from jax.experimental import pallas as pl
from jax.experimental.pallas import tpu as pltpu
from jax.sharding import PartitionSpec as P

coef = math.sqrt(2.0 / math.pi)
MESH = pl.DeviceIdType.MESH
BLOCKS = 1


def gelu_pair(pre):
    inner = coef * (pre + 0.044715 * pre * pre * pre)
    tanh_val = jnp.tanh(inner)
    value = 0.5 * pre * (1.0 + tanh_val)
    slope = 0.5 * (1.0 + tanh_val) + 0.5 * pre * (1.0 - tanh_val * tanh_val) * coef * (
        1.0 + 3.0 * 0.044715 * pre * pre
    )
    return (value, slope)


def contract_rows(left, right):
    return lax.dot_general(
        left, right, (((0,), (0,)), ((), ())), preferred_element_type=jnp.float32
    )


def contract_cols(left, right):
    return lax.dot_general(
        left, right, (((1,), (1,)), ((), ())), preferred_element_type=jnp.float32
    )


def flip(index, bits):
    bit = 1
    out = index
    while bit <= bits:
        if bits & bit:
            out = out + bit - 2 * bit * ((index // bit) % 2)
        bit *= 2
    return out


def exchange(
    n_dp, n_row, n_col,
    tok_ref, og_ref, len_ref, bias_ref, wup_hbm, wdn_hbm,
    ig_ref, feats_out, grads_out, act_out, pg_out,
    xg, wup, wdn, part, sent, core_in, mid, row_in, ap, igs, igf, x_in, zs, zr,
    w_sem, own_sem, out_sem, act_sem, ag_send_r, ag_send_l, ag_send_x, ag_recv,
    core_sem, row_sem, pair_sem, igx_send, igx_recv, z_send, z_recv,
):
    dp, row, col = lax.axis_index("dp"), lax.axis_index("row"), lax.axis_index("col")
    bl, width = tok_ref.shape
    blocks = len_ref.shape[0]
    hs = wup.shape[1]
    S = BLOCKS
    nch = n_col // S
    slab = n_dp * bl
    rows = S * slab
    half = rows // 2
    tile = min(256, hs)
    first = pl.multiple_of(dp * hs, hs)
    mate = flip(row, 1)
    mine = row % 2
    far_bits = [1 << b for b in range(1, n_row.bit_length() - 1)]
    pending = []

    w_copies = [
        pltpu.make_async_copy(wup_hbm.at[:, pl.ds(first, hs)], wup, w_sem.at[0]),
        pltpu.make_async_copy(wdn_hbm.at[pl.ds(first, hs), :], wdn, w_sem.at[1]),
    ]
    for copy in w_copies:
        copy.start()

    def group(g):
        return pl.ds(pl.multiple_of(g * bl, bl), bl)

    def block(k, c, g):
        return xg.at[k, c, group(g), :]

    barrier = pltpu.get_barrier_semaphore()
    peers = [{"dp": (dp + p) % n_dp} for p in range(1, n_dp)]
    peers += [{"row": mate}] + [{"row": flip(row, bits)} for bits in far_bits]
    for peer in peers:
        pl.semaphore_signal(barrier, inc=1, device_id=peer, device_id_type=MESH)
    has_r, has_l = col + 1 < n_col, col >= 1
    step_r, step_l = jnp.minimum(col + 1, n_col - 1), jnp.maximum(col - 1, 0)
    for cond, c in ((has_r, step_r), (has_l, step_l)):
        @pl.when(cond)
        def _():
            pl.semaphore_signal(barrier, inc=1, device_id={"col": c}, device_id_type=MESH)
    xg[0, col, group(dp), :] = tok_ref[...]
    spot = lax.broadcasted_iota(jnp.int32, (bl, width), 0)
    live = spot < len_ref[0]
    for k in range(1, blocks):
        start = k * (bl // blocks)
        live = jnp.where(spot < start, live, spot - start < len_ref[k])
    out_grad = og_ref[...].astype(jnp.float32)
    xg[1, col, group(dp), :] = jnp.where(live, out_grad, jnp.zeros_like(out_grad)).astype(jnp.bfloat16)
    beside = jnp.minimum(n_col - 1 - col, 1) + jnp.minimum(col, 1)
    pl.semaphore_wait(barrier, len(peers) + beside)

    def remote(src, dst, send, recv, dev):
        return pltpu.make_async_remote_copy(
            src_ref=src, dst_ref=dst, send_sem=send, recv_sem=recv,
            device_id=dev, device_id_type=MESH,
        )

    def go(copy, cond=None):
        if cond is None:
            copy.start()
        else:
            pl.when(cond)(copy.start)
        pending.append((copy, cond))

    def give(k, c, p):
        return remote(
            block(k, c, dp), block(k, c, dp), ag_send_x.at[k, p, c], ag_recv.at[k, dp, c],
            {"dp": (dp + p) % n_dp},
        )

    def arrived(k, c, g):
        return remote(block(k, c, g), block(k, c, g), own_sem, ag_recv.at[k, g, c], {"col": col})

    def forward(s):
        low = jnp.maximum(col - s, 0)
        high = jnp.minimum(col + s, n_col - 1)
        has_low, has_high = col - s >= 0, col + s < n_col
        for k in range(2):
            for c, cond, edge, to, sems in (
                (low, has_low, has_r, step_r, ag_send_r),
                (high, has_high, has_l, step_l, ag_send_l),
            ):
                if s > 0:
                    pl.when(cond)(arrived(k, c, dp).wait_recv)
                if s < n_col - 1:
                    go(remote(block(k, c, dp), block(k, c, dp), sems.at[k, s],
                              ag_recv.at[k, dp, c], {"col": to}), jnp.logical_and(cond, edge))
            if s == 0:
                for p in range(1, n_dp):
                    go(give(k, col, p))
            else:
                for c, cond in ((low, has_low), (high, has_high)):
                    for p in range(1, n_dp):
                        go(give(k, c, p), cond)

    forward(0)

    def base(j):
        return S * flip(col // S, j)

    def lanes(n):
        return pl.ds(pl.multiple_of(n * tile, tile), tile)

    def my_half(which):
        return pl.ds(pl.multiple_of(which * half, half), half)

    def stage_a(j):
        for i in range(S):
            c = base(j) + i
            for p in range(1, n_dp):
                g = (dp + p) % n_dp
                for k in range(2):
                    arrived(k, c, g).wait_recv()
        if j == 0:
            for copy in w_copies:
                copy.wait()
        b = base(j)

        @pl.loop(0, hs // tile)
        def _(n):
            feats = xg[0, pl.ds(b, S)].reshape(rows, width)
            grads = xg[1, pl.ds(b, S)].reshape(rows, width)
            up = jnp.dot(feats, wup[:, lanes(n)], preferred_element_type=jnp.float32)
            part[j, 0, :, lanes(n)] = up
            sent[j, 0, :, lanes(n)] = up.astype(jnp.bfloat16)
            down = contract_cols(grads, wdn[lanes(n), :])
            part[j, 1, :, lanes(n)] = down
            sent[j, 1, :, lanes(n)] = down.astype(jnp.bfloat16)

        go(remote(sent.at[j, :, my_half(1 - mine), :], core_in.at[j],
                  core_sem.at[0, j], core_sem.at[1, j], {"row": mate}))

    def stage_b(j):
        remote(core_in.at[j], core_in.at[j], own_sem, core_sem.at[1, j], {"row": mate}).wait_recv()

        @pl.loop(0, hs // tile)
        def _(n):
            for k in range(2):
                total = part[j, k, my_half(mine), lanes(n)] + core_in[j, k, :, lanes(n)].astype(jnp.float32)
                mid[j, 0, k, :, lanes(n)] = total.astype(jnp.bfloat16)

        go(remote(mid.at[j, 0], row_in.at[j, 0], row_sem.at[0, j, 0], row_sem.at[1, j, 0],
                  {"row": flip(row, far_bits[0])}))

    def stage_c(j):
        for i, bits in enumerate(far_bits):
            remote(row_in.at[j, i], row_in.at[j, i], own_sem, row_sem.at[1, j, i],
                   {"row": mate}).wait_recv()
            if i + 1 < len(far_bits):
                mid[j, i + 1] = (mid[j, i].astype(jnp.float32) + row_in[j, i].astype(jnp.float32)).astype(jnp.bfloat16)
                go(remote(mid.at[j, i + 1], row_in.at[j, i + 1], row_sem.at[0, j, i + 1],
                          row_sem.at[1, j, i + 1], {"row": flip(row, far_bits[i + 1])}))
        last = len(far_bits) - 1

        @pl.loop(0, hs // tile)
        def _(n):
            pre = mid[j, last, 0, :, lanes(n)].astype(jnp.float32) + row_in[j, last, 0, :, lanes(n)].astype(jnp.float32)
            grad = mid[j, last, 1, :, lanes(n)].astype(jnp.float32) + row_in[j, last, 1, :, lanes(n)].astype(jnp.float32)
            bias = bias_ref[:, pl.ds(pl.multiple_of(dp * hs + n * tile, tile), tile)]
            value, slope = gelu_pair(pre + bias)
            ap[0, j, my_half(mine), lanes(n)] = value.astype(jnp.bfloat16)
            ap[1, j, my_half(mine), lanes(n)] = (grad * slope).astype(jnp.bfloat16)

        here = ap.at[:, j, my_half(mine), :]
        go(remote(here, here, pair_sem.at[0, j], pair_sem.at[1, j], {"row": mate}))

    def stage_d(j):
        there = ap.at[:, j, my_half(1 - mine), :]
        remote(there, there, own_sem, pair_sem.at[1, j], {"row": mate}).wait_recv()
        wide = min(256, width)

        @pl.loop(0, width // wide)
        def _(n):
            cols = pl.ds(pl.multiple_of(n * wide, wide), wide)
            res = contract_cols(ap[1, j], wup[cols, :])
            for i in range(S):
                igf[j, i, :, cols] = res[i * slab : (i + 1) * slab]
                igs[j, i, :, cols] = res[i * slab : (i + 1) * slab].astype(jnp.bfloat16)

        for i in range(S):
            for p in range(1, n_dp):
                g = (dp + p) % n_dp
                go(remote(igs.at[j, i, group(g), :], x_in.at[j, p, i], igx_send.at[j, p, i],
                          igx_recv.at[j, p, i], {"dp": g}))

    def stage_e(j):
        for i in range(S):
            for p in range(1, n_dp):
                remote(x_in.at[j, p, i], x_in.at[j, p, i], own_sem, igx_recv.at[j, p, i], {"dp": dp}).wait_recv()
            total = igf[j, i, group(dp), :]
            for p in range(1, n_dp):
                total = total + x_in[j, p, i].astype(jnp.float32)
            if j == 0:
                igf[j, i, group(dp), :] = total
            if j > 0 or S > 1:
                zs[j, i] = total.astype(jnp.bfloat16)
                cond = i != col % S if j == 0 else None
                go(remote(zs.at[j, i], zr.at[col], z_send.at[j, i], z_recv.at[col], {"col": base(j) + i}), cond)

    out_copies = [
        pltpu.make_async_copy(xg.at[0], feats_out, out_sem.at[0]),
        pltpu.make_async_copy(xg.at[1], grads_out, out_sem.at[1]),
    ]
    act_copies = []
    for j in range(nch):
        at = base(j) // S
        act_copies.append(pltpu.make_async_copy(ap.at[0, j], act_out.at[at], act_sem.at[0, j]))
        act_copies.append(pltpu.make_async_copy(ap.at[1, j], pg_out.at[at], act_sem.at[1, j]))

    def finish(copies):
        for copy in copies:
            copy.start()

    steps = [(forward, s) for s in range(1, min(S + 1, n_col))]
    waits = [(forward, s) for s in range(S + 1, n_col)]
    for t in range(nch + 2):
        if t < nch:
            if t == nch - 1:
                steps += waits
                waits = []
            steps += [(stage_a, t)]
            steps += waits[:1]
            waits = waits[1:]
            if t == nch - 1:
                steps += [(finish, out_copies)]
        if 0 <= t - 1 < nch:
            steps += [(stage_c, t - 1)]
        if t < nch:
            steps += [(stage_b, t)]
        if 0 <= t - 1 < nch:
            steps += [(stage_d, t - 1), (finish, act_copies[2 * t - 2 : 2 * t])]
        if 0 <= t - 2 < nch:
            steps += [(stage_e, t - 2)]
    for step, *args in steps:
        step(*args)
    total = igf[0, col % S, group(dp), :]
    for p in range(1, n_col):
        c = (col + p) % n_col
        remote(zr.at[c], zr.at[c], own_sem, z_recv.at[c], {"col": c}).wait_recv()
        total = total + zr[c].astype(jnp.float32)
    ig_ref[...] = total.astype(jnp.bfloat16)
    for copy, cond in pending:
        if cond is None:
            copy.wait_send()
        else:
            pl.when(cond)(copy.wait_send)
    for copy in out_copies + act_copies:
        copy.wait()


def grads_kernel(feats_ref, pg_ref, act_ref, grads_ref, ig_ref, up_ref, bias_ref, down_ref, out_ref):
    @pl.when(pl.program_id(0) == 0)
    def _():
        bias_ref[...] = jnp.sum(pg_ref[...].astype(jnp.float32), axis=0, keepdims=True)
        out_ref[...] = ig_ref[...]

    hs = pg_ref.shape[1]
    up = contract_rows(feats_ref[...], pg_ref[...])
    for k in range(hs // 128):
        up_ref[:, k, :] = up[:, k * 128 : (k + 1) * 128]
    down_ref[0] = contract_rows(act_ref[...], grads_ref[...])


def weight_grads(feats, grads, act, pg, input_grad):
    rows, width = feats.shape
    hs = pg.shape[1]
    steps = max(1, hs // 512)
    f32 = jnp.float32
    return pl.pallas_call(
        grads_kernel,
        grid=(steps,),
        out_shape=(
            jax.ShapeDtypeStruct((width, hs // 128, 128), f32),
            jax.ShapeDtypeStruct((1, hs), f32),
            jax.ShapeDtypeStruct((1, hs, width), f32),
            jax.ShapeDtypeStruct(input_grad.shape, input_grad.dtype),
        ),
        in_specs=[
            pl.BlockSpec((rows, width // steps), lambda i: (0, i)),
            pl.BlockSpec((rows, hs), lambda i: (0, 0), pipeline_mode=pl.Buffered(1)),
            pl.BlockSpec((rows, hs // steps), lambda i: (0, i)),
            pl.BlockSpec((rows, width), lambda i: (0, 0), pipeline_mode=pl.Buffered(1)),
            pl.BlockSpec(input_grad.shape, lambda i: (0, 0), pipeline_mode=pl.Buffered(1)),
        ],
        out_specs=(
            pl.BlockSpec((width // steps, hs // 128, 128), lambda i: (i, 0, 0)),
            pl.BlockSpec((1, hs), lambda i: (0, 0)),
            pl.BlockSpec((1, hs // steps, width), lambda i: (0, i, 0)),
            pl.BlockSpec(input_grad.shape, lambda i: (0, 0)),
        ),
        compiler_params=pltpu.CompilerParams(vmem_limit_bytes=63 * 1024 * 1024),
    )(feats, pg, act, grads, input_grad)


def local(n_dp, n_row, n_col, tokens, up_weight, up_bias, down_weight, out_grad, bucket_lengths):
    bl, width = out_grad.shape
    hidden = up_weight.shape[1]
    hs = hidden // n_dp
    S = BLOCKS
    nch = n_col // S
    slab = n_dp * bl
    rows = S * slab
    far = n_row.bit_length() - 2
    bf, f32 = jnp.bfloat16, jnp.float32
    VM, DMA = pltpu.VMEM, pltpu.SemaphoreType.DMA
    vmem = pl.BlockSpec(memory_space=pltpu.VMEM)
    smem = pl.BlockSpec(memory_space=pltpu.SMEM)
    hbm = pl.BlockSpec(memory_space=pl.ANY)
    input_grad, feats, grads, act, pg = pl.pallas_call(
        functools.partial(exchange, n_dp, n_row, n_col),
        out_shape=(
            jax.ShapeDtypeStruct((bl, width), bf),
            jax.ShapeDtypeStruct((n_col, slab, width), bf),
            jax.ShapeDtypeStruct((n_col, slab, width), bf),
            jax.ShapeDtypeStruct((nch, rows, hs), bf),
            jax.ShapeDtypeStruct((nch, rows, hs), bf),
        ),
        in_specs=[vmem, vmem, smem, vmem, hbm, hbm],
        out_specs=(vmem, hbm, hbm, hbm, hbm),
        scratch_shapes=[
            VM((2, n_col, slab, width), bf),
            VM((width, hs), bf),
            VM((hs, width), bf),
            VM((nch, 2, rows, hs), f32),
            VM((nch, 2, rows, hs), bf),
            VM((nch, 2, rows // 2, hs), bf),
            VM((nch, far, 2, rows // 2, hs), bf),
            VM((nch, far, 2, rows // 2, hs), bf),
            VM((2, nch, rows, hs), bf),
            VM((nch, S, slab, width), bf),
            VM((nch, S, slab, width), f32),
            VM((nch, n_dp, S, bl, width), bf),
            VM((nch, S, bl, width), bf),
            VM((n_col, bl, width), bf),
            DMA((2,)), DMA(()), DMA((2,)), DMA((2, nch)),
            DMA((2, n_col)), DMA((2, n_col)), DMA((2, n_dp, n_col)), DMA((2, n_dp, n_col)),
            DMA((2, nch)), DMA((2, nch, far)), DMA((2, nch)),
            DMA((nch, n_dp, S)), DMA((nch, n_dp, S)), DMA((nch, S)), DMA((n_col,)),
        ],
        compiler_params=pltpu.CompilerParams(
            collective_id=0, has_side_effects=True, vmem_limit_bytes=60 * 1024 * 1024
        ),
    )(tokens, out_grad, bucket_lengths, up_bias.reshape(1, hidden), up_weight, down_weight)
    feats = feats.reshape(n_col * slab, width)
    grads = grads.reshape(n_col * slab, width)
    act = act.reshape(n_col * slab, hs)
    pg = pg.reshape(n_col * slab, hs)
    up_grad, bias_grad, down_grad, input_grad = weight_grads(feats, grads, act, pg, input_grad)
    return (
        input_grad,
        up_grad.reshape(width, 1, hs),
        bias_grad.reshape(1, hs),
        down_grad.reshape(1, hs, width),
    )


def solution(mesh):
    sizes = (mesh.shape["dp"], mesh.shape["row"], mesh.shape["col"])
    return jax.shard_map(
        functools.partial(local, *sizes),
        mesh=mesh,
        in_specs=(
            P(("dp", "col"), "row"),
            P("row", "col"),
            P("col"),
            P("col", "row"),
            P(("dp", "col"), "row"),
            P(("dp", "col")),
        ),
        out_specs=(
            P(("dp", "col"), "row"),
            P("row", "col", "dp"),
            P("col", "dp"),
            P("col", "dp", "row"),
        ),
        check_vma=False,
    )
```
